32 devices in a mesh: section: 2 (over core), blk: 8 (over z, y), head: 2 (over x).
Axes of the slice: x: 2, y: 2, z: 4, core: 2. Of those that a mesh axis runs over, the one named last changes fastest.
Arguments:
- projected: bfloat16 [8192, 8192], P(('section', 'blk')), may hold values from -6 to 6
- key_weight: bfloat16 [8192, 1024], P(None, 'head'), may hold values from -0.0625 to 0.0625
- value_weight: bfloat16 [8192, 1024], P(None, 'head'), may hold values from -0.0625 to 0.0625
- key_gain: float32 [128], replicated, may hold values from 0.1 to 1.9
- queries: bfloat16 [1024, 8, 1024], P('blk', 'section', 'head'), may hold values from -320 to 320
- frame_tokens: int32 [32], replicated, may hold values from 1 to 512, 8192 in all
- span_first: int32 [1024], replicated, may hold values from 0 to 31
- span_count: int32 [1024], replicated, may hold values from 1 to 32
Outputs:
- attended: bfloat16 [1024, 8, 1024], P('blk', 'section', 'head')
The draws below stay inside these ranges and needn't reach their ends.
Inputs may be any that keep to these rules, and one draw needn't show every extreme that they name: Frame f holds frame_tokens[f] consecutive visual tokens, and they sum to 8192.
All inputs are finite; a program needn't handle non-finite values.
Results may differ from the reference program's by a relative error of at most 0.005.
The reference program's roundings to bfloat16 on the way count: a program that leaves them out, or rounds other values in their place, can miss the bound.
Values may be sent and summed in bfloat16 or wider, within the bound.
No kernel may reach another device: no remote copies, remote signals or barrier semaphores. Data moves between devices by JAX's collectives and lax.ppermute only.
A program may use at most 192 MiB of HBM per device.

```python
import math
import jax
import jax.numpy as jnp
import numpy as np
from jax import lax

D = 8192
KV = 8
QPG = 8
HD = 128
FRAMES = 32
VT = 8192
QTOT = 1024
FMAX = 512


def draw_queries(key, part):
    normal_part = jax.random.normal(jax.random.fold_in(key, 11), (QTOT, QPG, KV * HD), jnp.float32)
    normal_part = jnp.clip(normal_part, -5.0, 5.0)
    return (normal_part * 2.5).astype(jnp.bfloat16)


def with_ends(values, own_key, low, high):
    dims = values.shape
    place = [jax.random.randint(jax.random.fold_in(own_key, axis), (), 0, dims[axis]) for axis in range(len(dims))]
    values = values.at[tuple(place)].set(low)
    longest = dims.index(max(dims))
    place[longest] = (place[longest] + 1) % dims[longest]
    return values.at[tuple(place)].set(high)


def shard_levels(stream_key, dims, shards, low, high):
    gain = 1.0
    for position, blocks in shards:
        steps = jax.random.uniform(jax.random.fold_in(jax.random.fold_in(stream_key, 6), position), (blocks,), jnp.float32, low / len(shards), high / len(shards))
        gain = gain * jnp.repeat(jnp.exp(steps), dims[position] // blocks).reshape((-1,) + (1,) * (len(dims) - 1 - position))
    return gain


def split_up(count, total, bound, slope):
    portions = [(1 << 20) // math.isqrt(rank ** slope) + 1 for rank in range(2, count + 1)]
    spare, counts = total - bound - (count - 1), [1] * (count - 1)
    while spare > 0:
        candidates = [i for i in range(count - 1) if counts[i] < bound]
        mass, budget = sum([portions[i] for i in candidates]), spare
        for i in candidates:
            addition = min(bound - counts[i], max(1, budget * portions[i] // mass), spare)
            counts[i] = counts[i] + addition
            spare = spare - addition
    return np.array([bound] + counts)


def uneven(own_key, count, total, reach, skew):
    if count == 2:
        one = jax.random.randint(own_key, (), max(1, total - reach), min(reach, total - 1) + 1)
        return jnp.stack([one, total - one])
    lengths = jnp.asarray(split_up(count, total, reach, skew), jnp.int32)
    couples = (count - 1) // 2
    source_of, sink = lengths[1:1 + 2 * couples:2], lengths[2:2 + 2 * couples:2]
    margin = jnp.minimum(source_of - 1, reach - sink)
    shifted = jax.random.randint(jax.random.fold_in(own_key, 1), (couples,), 0, 1 << 20) % (margin + 1)
    lengths = lengths.at[1:1 + 2 * couples:2].set(source_of - shifted).at[2:2 + 2 * couples:2].set(sink + shifted)
    return lengths[jax.random.permutation(jax.random.fold_in(own_key, 2), count)]


def gaussian(key, shape, deviation, reach, cuts=(), held_as=jnp.bfloat16):
    level = shard_levels(key, shape, cuts, -0.22, 0.18) if cuts else 1.0
    entries = jax.random.normal(key, shape, jnp.float32) * deviation * level
    return jnp.minimum(jnp.maximum(entries, -reach), reach).astype(held_as)


def setup_inputs(seed: int = 0) -> dict:
    streams_of = jax.random.split(jax.random.key(seed), 9)
    return {
        "projected": gaussian(streams_of[0], (VT, D), 1.0, 6.0, ((0, 16),)),
        "key_weight": gaussian(streams_of[1], (D, KV * HD), D ** -0.5, 0.0625, ((1, 2),)),
        "value_weight": gaussian(streams_of[2], (D, KV * HD), D ** -0.5, 0.0625, ((1, 2),)),
        "key_gain": jnp.clip(1.0 + 0.18 * jax.random.normal(streams_of[3], (HD,), jnp.float32), 0.1, 1.9),
        "queries": draw_queries(jax.random.fold_in(streams_of[8], 71), 0),
        "frame_tokens": uneven(streams_of[5], FRAMES, VT, FMAX, 1).astype(jnp.int32),
        "span_first": with_ends(jax.random.randint(streams_of[6], (QTOT,), 0, FRAMES), jax.random.fold_in(streams_of[6], 1), 0, FRAMES - 1).astype(jnp.int32),
        "span_count": with_ends(jax.random.randint(streams_of[7], (QTOT,), 1, FRAMES + 1), jax.random.fold_in(streams_of[7], 1), 1, FRAMES).astype(jnp.int32),
    }


def span_bounds(frame_tokens, span_first, span_count):
    frame_ids = jnp.arange(FRAMES, dtype=jnp.int32)
    span_end = jnp.minimum(span_first + span_count, FRAMES)
    first_token = lax.optimization_barrier(jnp.sum(jnp.where(frame_ids[None, :] < span_first[:, None], frame_tokens[None, :], 0), axis=1)).astype(jnp.int32)
    end_token = lax.optimization_barrier(jnp.sum(jnp.where(frame_ids[None, :] < span_end[:, None], frame_tokens[None, :], 0), axis=1)).astype(jnp.int32)
    return (first_token, end_token)

def reference(projected, key_weight, value_weight, key_gain, queries, frame_tokens, span_first, span_count):
    key_raw = jnp.dot(projected, key_weight, preferred_element_type=jnp.float32).reshape(VT, KV, HD)
    mean_square = lax.optimization_barrier(jnp.mean(key_raw * key_raw, axis=2, keepdims=True))
    key_table = (key_raw / jnp.sqrt(mean_square + 1e-05) * key_gain).astype(jnp.bfloat16)
    value_table = jnp.dot(projected, value_weight, preferred_element_type=jnp.float32).astype(jnp.bfloat16).reshape(VT, KV, HD)
    key_table = lax.optimization_barrier(key_table)
    value_table = lax.optimization_barrier(value_table)
    first_token, end_token = span_bounds(frame_tokens, span_first, span_count)
    positions = jnp.arange(VT, dtype=jnp.int32)
    block_rows = math.gcd(QTOT, 128)
    block_count = QTOT // block_rows
    keys_by_head = jnp.transpose(key_table, (1, 0, 2)).astype(jnp.float32)
    values_by_head = jnp.transpose(value_table, (1, 0, 2)).astype(jnp.float32)
    queries_by_head = jnp.transpose(queries.reshape(QTOT, QPG, KV, HD), (2, 0, 1, 3)).astype(jnp.float32)
    first_blocks = first_token.reshape(block_count, block_rows)
    end_blocks = end_token.reshape(block_count, block_rows)

    def per_head(operands):
        head_queries, head_keys, head_values = operands

        def per_block(block_operands):
            block_queries, block_first, block_end = block_operands
            scores = jnp.einsum('npd,md->npm', block_queries, head_keys) * HD ** (-0.5)
            allowed = (positions[None, :] >= block_first[:, None]) & (positions[None, :] < block_end[:, None])
            scores = jnp.where(allowed[:, None, :], scores, -1e+30)
            row_max = lax.optimization_barrier(jnp.max(scores, axis=2, keepdims=True))
            weights = jnp.exp(scores - row_max)
            denominator = lax.optimization_barrier(jnp.sum(weights, axis=2))
            rounded = lax.optimization_barrier(weights.astype(jnp.bfloat16)).astype(jnp.float32)
            numerator = jnp.einsum('npm,md->npd', rounded, head_values)
            return numerator / denominator[:, :, None]
        blocks = lax.map(per_block, (head_queries.reshape(block_count, block_rows, QPG, HD), first_blocks, end_blocks))
        return blocks.reshape(QTOT, QPG, HD)
    attended = lax.map(per_head, (queries_by_head, keys_by_head, values_by_head))
    return jnp.transpose(attended, (1, 2, 0, 3)).reshape(QTOT, QPG, KV * HD).astype(jnp.bfloat16)
```

```python
import functools
import math

import jax
import jax.numpy as jnp
from jax import lax
from jax.experimental import pallas as pl
from jax.experimental.pallas import tpu as pltpu
from jax.sharding import PartitionSpec as P

HD = 128
FRAMES = 32
EPS = 1e-05
MASKED = -1e30
EXP_SCALE = math.log2(math.e) * HD ** (-0.5)
MIB = 1 << 20
F32 = jnp.float32
BF16 = jnp.bfloat16


def project_kernel(steps, heads, x_ref, kw_ref, vw_ref, gain_ref, out_ref, k_acc, v_acc):
    step = pl.program_id(0)
    x = x_ref[...]
    k_part = jnp.dot(x, kw_ref[...], preferred_element_type=F32)
    v_part = jnp.dot(x, vw_ref[...], preferred_element_type=F32)

    @pl.when(step == 0)
    def _():
        k_acc[...] = k_part
        v_acc[...] = v_part

    @pl.when(step > 0)
    def _():
        k_acc[...] += k_part
        v_acc[...] += v_part

    @pl.when(step == steps - 1)
    def _():
        for head in range(heads):
            columns = slice(head * HD, (head + 1) * HD)
            raw = k_acc[:, columns]
            mean_square = jnp.mean(raw * raw, axis=1, keepdims=True)
            keys = raw / jnp.sqrt(mean_square + EPS) * gain_ref[...]
            out_ref[head, :, :HD] = keys.astype(BF16)
            out_ref[head, :, HD:] = v_acc[:, columns].astype(BF16)


def project(projected, key_weight, value_weight, gain, chunk, heads):
    rows, depth = projected.shape
    tile = min(1024, depth)
    steps = depth // tile
    width = heads * HD
    return pl.pallas_call(
        functools.partial(project_kernel, steps, heads),
        grid=(steps,),
        in_specs=[
            pl.BlockSpec((rows, tile), lambda k: (0, k)),
            pl.BlockSpec((tile, width), lambda k: (k, chunk)),
            pl.BlockSpec((tile, width), lambda k: (k, chunk)),
            pl.BlockSpec((1, HD), lambda k: (0, 0)),
        ],
        out_specs=pl.BlockSpec((heads, rows, 2 * HD), lambda k: (0, 0, 0)),
        out_shape=jax.ShapeDtypeStruct((heads, rows, 2 * HD), BF16),
        scratch_shapes=[pltpu.VMEM((rows, width), F32), pltpu.VMEM((rows, width), F32)],
        cost_estimate=pl.CostEstimate(
            flops=4 * rows * depth * width,
            bytes_accessed=2 * depth * (rows + 2 * width),
            transcendentals=0,
        ),
        compiler_params=pltpu.CompilerParams(vmem_limit_bytes=32 * MIB),
        name=f"project_{chunk}",
    )(projected, key_weight, value_weight, gain)


def diagonal():
    rows = lax.broadcasted_iota(jnp.int32, (HD, HD), 0)
    lanes = lax.broadcasted_iota(jnp.int32, (HD, HD), 1)
    return rows == lanes


def to_lanes(column_block, eye):
    return jnp.sum(jnp.where(eye, column_block, 0.0), axis=0, keepdims=True)


def to_column(lane_row, eye):
    return jnp.sum(jnp.where(eye, lane_row, 0.0), axis=1, keepdims=True)


def split_rows(rows):
    high = rows.astype(BF16)
    rest = rows - high.astype(F32)
    middle = rest.astype(BF16)
    low = (rest - middle.astype(F32)).astype(BF16)
    return high, middle, low


def attend_kernel(groups, sources, packed, *refs):
    q_refs = refs[:groups]
    mask_ref = refs[groups]
    kv_refs = refs[groups + 1 : groups + 1 + sources]
    frames_ref, out_ref, keys, values = refs[groups + 1 + sources :]
    rows = q_refs[0].shape[0]
    count = kv_refs[0].shape[1]
    tile = min(256, rows)

    @pl.when(pl.program_id(0) == 0)
    def _():
        values[:, HD:] = jnp.ones((sources * count, HD), BF16)
        for source in range(sources):
            keys[source * count : (source + 1) * count, HD:] = frames_ref[source]

    for source in range(sources):
        span = slice(source * count, (source + 1) * count)
        keys[span, :HD] = kv_refs[source][0, :, :HD]
        values[span, :HD] = kv_refs[source][0, :, HD:]
    eye = diagonal()
    for group in range(groups):
        lane_rows = []
        for start in range(0, rows, tile):
            span = slice(start, start + tile)
            query = jnp.concatenate([q_refs[group][span, :], mask_ref[group, span, :]], axis=1)
            scores = lax.dot_general(
                query, keys[...], (((1,), (1,)), ((), ())), preferred_element_type=F32
            )
            row_max = jnp.max(scores, axis=1, keepdims=True)
            weights = jnp.exp2((scores - row_max) * EXP_SCALE).astype(BF16)
            summed = jnp.dot(weights, values[...], preferred_element_type=F32)
            denominator = summed[:, HD:]
            out_ref[group, 0, span, :] = (summed[:, :HD] / denominator).astype(out_ref.dtype)
            log_sum = row_max * EXP_SCALE + jnp.log2(denominator)
            for part in range(0, tile, HD):
                lane_rows.append(to_lanes(log_sum[part : part + HD], eye))
        store_lanes(out_ref, (group, 0), rows, lane_rows, packed)


def store_lanes(out_ref, lead, rows, lane_rows, packed):
    flat = jnp.concatenate(lane_rows, axis=0)
    count = flat.shape[0]
    pad = jnp.zeros((tail_rows(rows, packed) - (3 if packed else 1) * count, HD), F32)
    if packed:
        high, middle, low = split_rows(flat)
        flat = jnp.concatenate(
            [high.astype(F32), middle.astype(F32), low.astype(F32), pad], axis=0
        )
    else:
        flat = jnp.concatenate([flat, pad], axis=0) if pad.shape[0] else flat
    out_ref[lead[0], lead[1], rows:, :] = flat.astype(out_ref.dtype)


def load_lanes(ref, lead, rows, packed):
    flat = ref[lead[0], lead[1], rows:, :].astype(F32)
    count = rows // HD
    if packed:
        return flat[:count] + flat[count : 2 * count] + flat[2 * count : 3 * count]
    return flat[:count]


def tail_rows(rows, packed):
    count = rows // HD
    if packed:
        return -(-3 * count // 16) * 16
    return -(-count // 8) * 8


def attend(queries, mask, kv_sources, frames, packed, name):
    groups = len(queries)
    sources = len(kv_sources)
    heads, count, _ = kv_sources[0].shape
    rows = queries[0][0].shape[0]
    dtype = BF16 if packed else F32
    out_rows = rows + tail_rows(rows, packed)

    def column(offset):
        return lambda head: (0, offset + head)

    return pl.pallas_call(
        functools.partial(attend_kernel, groups, sources, packed),
        grid=(heads,),
        in_specs=[pl.BlockSpec((rows, HD), column(offset)) for _, offset in queries]
        + [pl.BlockSpec(mask.shape, lambda head: (0, 0, 0))]
        + [pl.BlockSpec((1, count, 2 * HD), lambda head: (head, 0, 0))] * sources
        + [pl.BlockSpec(frames.shape, lambda head: (0, 0, 0))],
        out_specs=pl.BlockSpec((groups, 1, out_rows, HD), lambda head: (0, head, 0, 0)),
        out_shape=jax.ShapeDtypeStruct((groups, heads, out_rows, HD), dtype),
        scratch_shapes=[
            pltpu.VMEM((sources * count, 2 * HD), BF16),
            pltpu.VMEM((sources * count, 2 * HD), BF16),
        ],
        cost_estimate=pl.CostEstimate(
            flops=8 * groups * heads * rows * sources * count * HD,
            bytes_accessed=heads * (sources * count * 512 + groups * rows * 512),
            transcendentals=groups * heads * rows * sources * count,
        ),
        compiler_params=pltpu.CompilerParams(vmem_limit_bytes=48 * MIB),
        name=name,
    )(*[array for array, _ in queries], mask, *kv_sources, frames)


def merge_pair(first, second, first_lanes, second_lanes, eye):
    top = jnp.maximum(first_lanes, second_lanes)
    first_weight = jnp.exp2(first_lanes - top)
    second_weight = jnp.exp2(second_lanes - top)
    total = first_weight + second_weight
    share = to_column(first_weight / total, eye)
    return share * first + (1.0 - share) * second, top + jnp.log2(total)


def merge_kernel(got_ref, own_ref, send_ref, keep_ref):
    groups, heads, rows_all, _ = got_ref.shape
    half = groups // 2
    rows = send_ref.shape[2] - tail_of(send_ref.shape[2], True)
    eye = diagonal()
    for group in range(groups):
        out_ref, place, packed = (keep_ref, group, False) if group < half else (
            send_ref,
            group - half,
            True,
        )
        for head in range(heads):
            got_lanes = load_lanes(got_ref, (group, head), rows, True)
            own_lanes = load_lanes(own_ref, (group, head), rows, False)
            lanes = []
            for index in range(rows // HD):
                span = slice(index * HD, (index + 1) * HD)
                merged, merged_lanes = merge_pair(
                    got_ref[group, head, span, :].astype(F32),
                    own_ref[group, head, span, :],
                    got_lanes[index : index + 1],
                    own_lanes[index : index + 1],
                    eye,
                )
                out_ref[place, head, span, :] = merged.astype(out_ref.dtype)
                lanes.append(merged_lanes)
            store_lanes(out_ref, (place, head), rows, lanes, packed)


def tail_of(total, packed):
    for rows in range(HD, total, HD):
        if rows + tail_rows(rows, packed) == total:
            return total - rows
    raise ValueError("rows")


def merge(got, own, name):
    groups, heads, packed_rows, _ = got.shape
    half = groups // 2
    return pl.pallas_call(
        merge_kernel,
        out_shape=(
            jax.ShapeDtypeStruct((half, heads, packed_rows, HD), BF16),
            jax.ShapeDtypeStruct((half, heads, own.shape[2], HD), F32),
        ),
        cost_estimate=pl.CostEstimate(
            flops=8 * own.size, bytes_accessed=12 * own.size, transcendentals=0
        ),
        compiler_params=pltpu.CompilerParams(vmem_limit_bytes=32 * MIB),
        name=name,
    )(got, own)


def finish_kernel(chunks, *refs):
    out_ref = refs[-1]
    rows = out_ref.shape[0]
    eye = diagonal()
    for chunk in range(chunks):
        got_ref, own_ref = refs[2 * chunk : 2 * chunk + 2]
        heads = own_ref.shape[1]
        for head in range(heads):
            got_lanes = load_lanes(got_ref, (0, head), rows, True)
            own_lanes = load_lanes(own_ref, (0, head), rows, False)
            column = (chunk * heads + head) * HD
            for index in range(rows // HD):
                span = slice(index * HD, (index + 1) * HD)
                merged, _ = merge_pair(
                    got_ref[0, head, span, :].astype(F32),
                    own_ref[0, head, span, :],
                    got_lanes[index : index + 1],
                    own_lanes[index : index + 1],
                    eye,
                )
                out_ref[span, column : column + HD] = merged.astype(BF16)


def finish(pairs, rows):
    heads = sum(own.shape[1] for _, own in pairs)
    return pl.pallas_call(
        functools.partial(finish_kernel, len(pairs)),
        out_shape=jax.ShapeDtypeStruct((rows, heads * HD), BF16),
        cost_estimate=pl.CostEstimate(
            flops=8 * rows * heads * HD, bytes_accessed=8 * rows * heads * HD, transcendentals=0
        ),
        compiler_params=pltpu.CompilerParams(vmem_limit_bytes=32 * MIB),
        name="finish",
    )(*[array for pair in pairs for array in pair])


def frame_starts(frame_tokens):
    ids = jnp.arange(FRAMES, dtype=jnp.int32)
    before = jnp.where(ids[:, None] < ids[None, :], frame_tokens[:, None], 0)
    return jnp.sum(before, axis=0)


def source_frames(starts, frame_tokens, block, count):
    positions = block * count + jnp.arange(count, dtype=jnp.int32)
    inside = (positions[:, None] >= starts[None, :]) & (
        positions[:, None] < (starts + frame_tokens)[None, :]
    )
    return jnp.pad(inside.astype(BF16), ((0, 0), (0, HD - FRAMES)))


def allowed_frames(span_first, span_count, block, own_rows, sub_heads):
    first = lax.dynamic_slice_in_dim(span_first, block * own_rows, own_rows)[:, None]
    end = jnp.minimum(
        first + lax.dynamic_slice_in_dim(span_count, block * own_rows, own_rows)[:, None], FRAMES
    )
    ids = jnp.arange(HD, dtype=jnp.int32)[None, :]
    blocked = jnp.where((ids >= FRAMES) | ((ids >= first) & (ids < end)), 0.0, MASKED)
    wide = jnp.broadcast_to(blocked.astype(BF16)[:, None, :], (own_rows, sub_heads, HD))
    return wide.reshape(own_rows * sub_heads, HD)


def body(
    projected, key_weight, value_weight, key_gain, queries, frame_tokens, span_first, span_count
):
    own_rows, sub_heads, width = queries.shape
    local_heads = width // HD
    count = projected.shape[0]
    chunk_heads = 2 if local_heads % 2 == 0 else 1
    chunks = local_heads // chunk_heads
    section_count = lax.axis_size("section")
    block_count = lax.axis_size("blk")
    section = lax.axis_index("section")
    block = lax.axis_index("blk")
    bits = block_count.bit_length() - 1
    near, far = 1, 1 << (bits - 1)
    middle = [1 << bit for bit in range(1, bits - 1)]

    def across(x, bit):
        return lax.ppermute(x, "blk", [(i, i ^ bit) for i in range(block_count)])

    def across_section(x):
        return lax.ppermute(
            x, "section", [(i, (i + 1) % section_count) for i in range(section_count)]
        )

    rows = own_rows * sub_heads
    shaped = queries.reshape(rows, width)
    chunk_width = chunk_heads * HD
    far_queries = [
        across(shaped[:, c * chunk_width : (c + 1) * chunk_width], far) for c in range(chunks)
    ]
    near_queries = across(shaped, near)
    near_far_queries = [across(part, near) for part in far_queries]

    starts = frame_starts(frame_tokens)
    source_bits = [0]
    for bit in middle:
        source_bits = source_bits + [other ^ bit for other in source_bits]
    places = [(s, other) for other in source_bits for s in range(section_count)]
    frames = jnp.stack(
        [
            source_frames(
                starts,
                frame_tokens,
                lax.rem(section + section_count - s, section_count) * block_count + (block ^ other),
                count,
            )
            for s, other in places
        ]
    )

    def masks(bits_of):
        return jnp.stack(
            [
                allowed_frames(span_first, span_count, block ^ other, own_rows, sub_heads)
                for other in bits_of
            ]
        )

    away_mask = masks([near, near ^ far])
    home_mask = masks([0, far])
    gain = key_gain.reshape(1, HD)

    received = []
    for c in range(chunks):
        own = project(projected, key_weight, value_weight, gain, c, chunk_heads)
        plane = [own]
        for bit in middle:
            plane = plane + [across(part, bit) for part in plane]
        kv_sources = []
        for part in plane:
            kv_sources.append(part)
            if section_count > 1:
                kv_sources.append(across_section(part))
        received.append(kv_sources)

    pairs = []
    for c in range(chunks):
        offset = c * chunk_heads
        away = attend(
            [(near_queries, offset), (near_far_queries[c], 0)],
            away_mask,
            received[c],
            frames,
            True,
            f"attend_away_{c}",
        )
        got = across(away, near)
        home = attend(
            [(shaped, offset), (far_queries[c], 0)],
            home_mask,
            received[c],
            frames,
            False,
            f"attend_home_{c}",
        )
        send, keep = merge(got, home, f"merge_{c}")
        pairs.append((across(send, far), keep))
    return finish(pairs, rows).reshape(own_rows, sub_heads, width)


def solution(mesh):
    placed = (
        P(("section", "blk"), None),
        P(None, "head"),
        P(None, "head"),
        P(),
        P("blk", "section", "head"),
        P(),
        P(),
        P(),
    )
    return jax.shard_map(
        body, mesh=mesh, in_specs=placed, out_specs=P("blk", "section", "head"), check_vma=False
    )
```

```python
import functools
import math

import jax
import jax.numpy as jnp
from jax import lax
from jax.experimental import pallas as pl
from jax.experimental.pallas import tpu as pltpu
from jax.sharding import PartitionSpec as P


HD = 128
FRAMES = 32
EPS = 1e-05
MASKED = -1e30
EXP_SCALE = math.log2(math.e) * HD ** (-0.5)
MIB = 1 << 20
F32 = jnp.float32
BF16 = jnp.bfloat16


def project_kernel(steps, heads, chunk, fetch, *refs):
    x_from, kw_from, vw_from, gain_ref, out_ref = refs[:5]
    x_ref = refs[5] if fetch else x_from
    kw_ref, vw_ref, k_acc, v_acc, sems = refs[6 if fetch else 5 :]
    depth, width = kw_ref.shape
    tile = depth // steps
    columns = pl.ds(chunk * width, width)
    copies = []
    for step in range(steps):
        span = pl.ds(step * tile, tile)
        group = [
            pltpu.make_async_copy(kw_from.at[span, columns], kw_ref.at[span], sems.at[0, step]),
            pltpu.make_async_copy(vw_from.at[span, columns], vw_ref.at[span], sems.at[1, step]),
        ]
        if fetch:
            group.append(
                pltpu.make_async_copy(x_from.at[:, span], x_ref.at[:, span], sems.at[2, step])
            )
        for copy in group:
            copy.start()
        copies.append(group)
    for step in range(steps):
        for copy in copies[step]:
            copy.wait()
        span = slice(step * tile, (step + 1) * tile)
        x = x_ref[:, span]
        k_part = jnp.dot(x, kw_ref[span], preferred_element_type=F32)
        v_part = jnp.dot(x, vw_ref[span], preferred_element_type=F32)
        if step == 0:
            k_acc[...] = k_part
            v_acc[...] = v_part
        else:
            k_acc[...] += k_part
            v_acc[...] += v_part
    for head in range(heads):
        columns = slice(head * HD, (head + 1) * HD)
        raw = k_acc[:, columns]
        mean_square = jnp.mean(raw * raw, axis=1, keepdims=True)
        keys = raw / jnp.sqrt(mean_square + EPS) * gain_ref[...]
        out_ref[head, :, :HD] = keys.astype(BF16)
        out_ref[head, :, HD:] = v_acc[:, columns].astype(BF16)


def project(projected, key_weight, value_weight, gain, chunk, heads, held, keep):
    rows, depth = projected.shape
    steps = 8
    width = heads * HD
    fetch = held is None
    vmem = pl.BlockSpec(memory_space=pltpu.VMEM)
    hbm = pl.BlockSpec(memory_space=pltpu.HBM)
    shape = jax.ShapeDtypeStruct((heads, rows, 2 * HD), BF16)
    x_space = pltpu.VMEM((rows, depth), BF16)
    result = pl.pallas_call(
        functools.partial(project_kernel, steps, heads, chunk, fetch),
        in_specs=[hbm if fetch else vmem, hbm, hbm, vmem],
        out_specs=(vmem, vmem) if keep else vmem,
        out_shape=(shape, x_space) if keep else shape,
        scratch_shapes=([x_space] if fetch and not keep else [])
        + [pltpu.VMEM((depth, width), BF16)] * 2
        + [pltpu.VMEM((rows, width), F32)] * 2
        + [pltpu.SemaphoreType.DMA((3, steps))],
        cost_estimate=pl.CostEstimate(
            flops=4 * rows * depth * width,
            bytes_accessed=2 * depth * (rows * fetch + 2 * width),
            transcendentals=0,
        ),
        compiler_params=pltpu.CompilerParams(vmem_limit_bytes=(50 if fetch else 40) * MIB),
    )(projected if fetch else held, key_weight, value_weight, gain)
    return result if keep else (result, held)


def diagonal():
    rows = lax.broadcasted_iota(jnp.int32, (HD, HD), 0)
    lanes = lax.broadcasted_iota(jnp.int32, (HD, HD), 1)
    return rows == lanes


def to_lanes(column_block, eye):
    return jnp.sum(jnp.where(eye, column_block, 0.0), axis=0, keepdims=True)


def to_column(lane_row, eye):
    return jnp.sum(jnp.where(eye, lane_row, 0.0), axis=1, keepdims=True)


def split_rows(rows):
    high = rows.astype(BF16)
    rest = rows - high.astype(F32)
    middle = rest.astype(BF16)
    low = (rest - middle.astype(F32)).astype(BF16)
    return high, middle, low


def attend_kernel(jobs, mask_count, chunks, sources, heads, *refs):
    group_count = len({group for group, _, _, _ in jobs})
    q_count = 1 + max(query for _, query, _, _ in jobs)
    q_refs, refs = refs[:q_count], refs[q_count:]
    mask_refs, refs = refs[:mask_count], refs[mask_count:]
    kv_refs, refs = refs[: chunks * sources], refs[chunks * sources :]
    frames_ref, refs = refs[0], refs[1:]
    out_refs, (keys, values, *buffers) = refs[:group_count], refs[group_count:]
    rows = q_refs[0].shape[0]
    count = kv_refs[0].shape[1]
    total = sources * count
    tile = min(256, rows)
    block = math.gcd(512, total)

    for slot in range(chunks * heads):
        chunk, head = divmod(slot, heads)
        values[slot, :, HD:] = jnp.ones((total, HD), BF16)
        for source in range(sources):
            span = slice(source * count, (source + 1) * count)
            kv = kv_refs[chunk * sources + source]
            keys[slot, span, :HD] = kv[head, :, :HD]
            keys[slot, span, HD:] = frames_ref[source]
            values[slot, span, :HD] = kv[head, :, HD:]

    eye = diagonal()
    tiles = [
        (group, query, mask, chunk, head, start)
        for group, query, mask, chunk in jobs
        for head in range(heads)
        for start in range(0, rows, tile)
    ]
    lane_rows = {}

    def load_query(index):
        _, query, mask, _, head, start = tiles[index]
        span = slice(start, start + tile)
        columns = slice(head * HD, (head + 1) * HD)
        return jnp.concatenate([q_refs[query][span, columns], mask_refs[mask][span, :]], axis=1)

    def score(index, begin, query):
        _, _, _, chunk, head, _ = tiles[index]
        span = slice(begin, begin + block)
        scores = lax.dot_general(
            query,
            keys[chunk * heads + head, span],
            (((1,), (1,)), ((), ())),
            preferred_element_type=F32,
        )
        buffers[index % 2][:, span] = scores
        top = scores[:, :HD]
        for part in range(HD, block, HD):
            top = jnp.maximum(top, scores[:, part : part + HD])
        return top

    def weigh(index, begin, row_max):
        _, _, _, chunk, head, _ = tiles[index]
        span = slice(begin, begin + block)
        weights = jnp.exp2((buffers[index % 2][:, span] - row_max) * EXP_SCALE)
        return jnp.dot(
            weights.astype(BF16), values[chunk * heads + head, span], preferred_element_type=F32
        )

    def store(index, summed, row_max):
        group, _, _, chunk, head, start = tiles[index]
        out_ref = out_refs[group]
        slot = chunk * heads + head if out_ref.shape[0] > heads else head
        denominator = summed[:, HD:]
        out_ref[slot, start : start + tile, :] = (summed[:, :HD] / denominator).astype(
            out_ref.dtype
        )
        log_sum = row_max * EXP_SCALE + jnp.log2(denominator)
        lanes = lane_rows.setdefault((group, slot), [])
        for part in range(0, tile, HD):
            lanes.append(to_lanes(log_sum[part : part + HD], eye))
        if len(lanes) * HD == rows:
            store_lanes(out_ref, slot, rows, lanes)

    top = None
    query = load_query(0)
    for begin in range(0, total, block):
        part = score(0, begin, query)
        top = part if top is None else jnp.maximum(top, part)
    for index in range(len(tiles)):
        row_max = jnp.max(top, axis=1, keepdims=True)
        ahead = index + 1 < len(tiles)
        if ahead:
            query = load_query(index + 1)
        top = summed = None
        for begin in range(0, total, block):
            if ahead:
                part = score(index + 1, begin, query)
                top = part if top is None else jnp.maximum(top, part)
            part = weigh(index, begin, row_max)
            summed = part if summed is None else summed + part
        store(index, summed, row_max)


def store_lanes(out_ref, slot, rows, lane_rows):
    packed = out_ref.dtype == BF16
    flat = jnp.concatenate(lane_rows, axis=0)
    pieces = [flat]
    if packed:
        pieces = [piece.astype(F32) for piece in split_rows(flat)]
    pad = tail_rows(rows, packed) - len(pieces) * flat.shape[0]
    if pad:
        pieces.append(jnp.zeros((pad, HD), F32))
    out_ref[slot, rows:, :] = jnp.concatenate(pieces, axis=0).astype(out_ref.dtype)


def load_lanes(ref, slot, rows):
    flat = ref[slot, rows:, :].astype(F32)
    count = rows // HD
    if ref.dtype == BF16:
        return flat[:count] + flat[count : 2 * count] + flat[2 * count : 3 * count]
    return flat[:count]


def tail_rows(rows, packed):
    count = rows // HD
    if packed:
        return -(-3 * count // 16) * 16
    return -(-count // 8) * 8


def attend(groups, kv_chunks, frames):
    chunks, sources = len(kv_chunks), len(kv_chunks[0])
    heads, count, _ = kv_chunks[0][0].shape
    rows = groups[0][0][0].shape[0]
    tile = min(256, rows)
    total = sources * count
    jobs, queries = [], []
    for group, (parts, _, _) in enumerate(groups):
        for chunk, part in enumerate(parts):
            jobs.append((group, len(queries), group, chunk))
            queries.append(part)
    slots = chunks * heads
    vmem = pl.BlockSpec(memory_space=pltpu.VMEM)
    inputs = [*queries, *[mask for _, mask, _ in groups], *sum(kv_chunks, []), frames]
    return pl.pallas_call(
        functools.partial(attend_kernel, tuple(jobs), len(groups), chunks, sources, heads),
        in_specs=[vmem] * len(inputs),
        out_specs=[vmem] * len(groups),
        out_shape=[
            jax.ShapeDtypeStruct(
                (slots, rows + tail_rows(rows, packed), HD), BF16 if packed else F32
            )
            for _, _, packed in groups
        ],
        scratch_shapes=[pltpu.VMEM((slots, total, 2 * HD), BF16)] * 2
        + [pltpu.VMEM((tile, total), F32)] * 2,
        cost_estimate=pl.CostEstimate(
            flops=8 * len(groups) * slots * rows * total * HD,
            bytes_accessed=slots * (total * 512 + len(groups) * rows * 512),
            transcendentals=len(groups) * slots * rows * total,
        ),
        compiler_params=pltpu.CompilerParams(vmem_limit_bytes=32 * MIB),
    )(*inputs)


def merge_lanes(lanes):
    top = functools.reduce(jnp.maximum, lanes)
    weights = [jnp.exp2(lane - top) for lane in lanes]
    total = functools.reduce(jnp.add, weights)
    return [weight / total for weight in weights], top + jnp.log2(total)


def merge_slot(refs, slots, rows, eye, write):
    lanes = [load_lanes(ref, slot, rows) for ref, slot in zip(refs, slots)]
    shares, merged_lanes = merge_lanes(lanes)
    for index in range(rows // HD):
        span = slice(index * HD, (index + 1) * HD)
        merged = None
        for ref, slot, share in zip(refs, slots, shares):
            part = to_column(share[index : index + 1], eye) * ref[slot, span, :].astype(F32)
            merged = part if merged is None else merged + part
        write(span, merged)
    return merged_lanes


def merge_kernel(rows, got_ref, own_ref, send_ref):
    eye = diagonal()
    for head in range(send_ref.shape[0]):

        def write(span, merged):
            send_ref[head, span, :] = merged.astype(BF16)

        lanes = merge_slot((got_ref, own_ref), (head, head), rows, eye, write)
        store_lanes(send_ref, head, rows, [lanes])


def merge(got, own, rows):
    return pl.pallas_call(
        functools.partial(merge_kernel, rows),
        out_shape=jax.ShapeDtypeStruct(got.shape, BF16),
        cost_estimate=pl.CostEstimate(
            flops=8 * own.size, bytes_accessed=8 * own.size, transcendentals=0
        ),
        compiler_params=pltpu.CompilerParams(vmem_limit_bytes=32 * MIB),
    )(got, own)


def finish_kernel(chunks, rows, own_ref, *refs):
    out_ref = refs[-1]
    eye = diagonal()
    sub_heads = out_ref.shape[1]
    for slot in range(own_ref.shape[0]):
        chunk, head = divmod(slot, own_ref.shape[0] // chunks)
        columns = slice(slot * HD, (slot + 1) * HD)

        def write(span, merged):
            texts = slice(span.start // sub_heads, span.stop // sub_heads)
            out_ref[texts, :, columns] = merged.reshape(-1, sub_heads, HD).astype(BF16)

        parts = (own_ref, refs[2 * chunk], refs[2 * chunk + 1])
        merge_slot(parts, (slot, head, head), rows, eye, write)


def finish(own, received, rows, shape):
    return pl.pallas_call(
        functools.partial(finish_kernel, len(received), rows),
        out_shape=jax.ShapeDtypeStruct(shape, BF16),
        cost_estimate=pl.CostEstimate(
            flops=8 * own.size, bytes_accessed=8 * own.size, transcendentals=0
        ),
        compiler_params=pltpu.CompilerParams(vmem_limit_bytes=32 * MIB),
        name="finish",
    )(own, *[array for pair in received for array in pair])


def frame_starts(frame_tokens):
    ids = jnp.arange(FRAMES, dtype=jnp.int32)
    before = jnp.where(ids[:, None] < ids[None, :], frame_tokens[:, None], 0)
    return jnp.sum(before, axis=0)


def source_frames(starts, frame_tokens, block, count):
    positions = block * count + jnp.arange(count, dtype=jnp.int32)
    inside = (positions[:, None] >= starts[None, :]) & (
        positions[:, None] < (starts + frame_tokens)[None, :]
    )
    return jnp.pad(inside.astype(BF16), ((0, 0), (0, HD - FRAMES)))


def allowed_frames(span_first, span_count, block, own_rows, sub_heads):
    first = lax.dynamic_slice_in_dim(span_first, block * own_rows, own_rows)[:, None]
    end = jnp.minimum(
        first + lax.dynamic_slice_in_dim(span_count, block * own_rows, own_rows)[:, None], FRAMES
    )
    ids = jnp.arange(HD, dtype=jnp.int32)[None, :]
    blocked = jnp.where((ids >= FRAMES) | ((ids >= first) & (ids < end)), 0.0, MASKED)
    wide = jnp.broadcast_to(blocked.astype(BF16)[:, None, :], (own_rows, sub_heads, HD))
    return wide.reshape(own_rows * sub_heads, HD)


def body(
    projected, key_weight, value_weight, key_gain, queries, frame_tokens, span_first, span_count
):
    own_rows, sub_heads, width = queries.shape
    local_heads = width // HD
    count = projected.shape[0]
    chunk_heads = 2 if local_heads % 2 == 0 else 1
    chunks = local_heads // chunk_heads
    section_count = lax.axis_size("section")
    block_count = lax.axis_size("blk")
    section = lax.axis_index("section")
    block = lax.axis_index("blk")
    bits = block_count.bit_length() - 1
    near, far = 1, 1 << (bits - 1)
    middle = [1 << bit for bit in range(1, bits - 1)]

    def across(x, bit):
        return lax.ppermute(x, "blk", [(i, i ^ bit) for i in range(block_count)])

    def across_section(x):
        return lax.ppermute(
            x, "section", [(i, (i + 1) % section_count) for i in range(section_count)]
        )

    rows = own_rows * sub_heads
    chunk_width = chunk_heads * HD
    own_queries = [
        queries[:, :, c * chunk_width : (c + 1) * chunk_width].reshape(rows, chunk_width)
        for c in range(chunks)
    ]
    far_queries, near_queries, near_far_queries = [], [], []
    for c in range(chunks):
        far_queries.append(across(own_queries[c], far))
        near_queries.append(across(own_queries[c], near))
    for c in range(chunks):
        near_far_queries.append(across(far_queries[c], near))

    starts = frame_starts(frame_tokens)
    source_bits = [0]
    for bit in middle:
        source_bits = source_bits + [other ^ bit for other in source_bits]
    places = [(s, other) for other in source_bits for s in range(section_count)]
    frames = jnp.stack(
        [
            source_frames(
                starts,
                frame_tokens,
                lax.rem(section + section_count - s, section_count) * block_count + (block ^ other),
                count,
            )
            for s, other in places
        ]
    )

    def mask(other):
        return allowed_frames(span_first, span_count, block ^ other, own_rows, sub_heads)

    gain = key_gain.reshape(1, HD)

    received = []
    held = None
    for c in range(chunks):
        own, held = project(
            projected, key_weight, value_weight, gain, c, chunk_heads, held, chunks > 1 and c == 0
        )
        plane = [own]
        for bit in middle:
            plane = plane + [across(part, bit) for part in plane]
        kv_sources = []
        for part in plane:
            kv_sources.append(part)
            if section_count > 1:
                kv_sources.append(across_section(part))
        received.append(kv_sources)

    got_back = []
    for c in range(chunks):
        (corner,) = attend([([near_far_queries[c]], mask(near ^ far), True)], [received[c]], frames)
        got_corner = across(corner, near)
        far_side, near_side = attend(
            [([far_queries[c]], mask(far), False), ([near_queries[c]], mask(near), True)],
            [received[c]],
            frames,
        )
        got_near = across(near_side, near)
        send = merge(got_corner, far_side, rows)
        got_back.append((got_near, across(send, far)))
    (home,) = attend([(own_queries, mask(0), False)], received, frames)
    return finish(home, got_back, rows, queries.shape)


def solution(mesh):
    placed = (
        P(("section", "blk"), None),
        P(None, "head"),
        P(None, "head"),
        P(),
        P("blk", "section", "head"),
        P(),
        P(),
        P(),
    )
    return jax.shard_map(
        body,
        mesh=mesh,
        in_specs=placed,
        out_specs=P("blk", "section", "head"),
        check_vma=False,
    )
```

```python
import functools
import math

import jax
import jax.numpy as jnp
from jax import lax
from jax.experimental import pallas as pl
from jax.experimental.pallas import tpu as pltpu
from jax.sharding import PartitionSpec as P


HD = 128
FRAMES = 32
EPS = 1e-05
MASKED = -1e30
EXP_SCALE = math.log2(math.e) * HD ** (-0.5)
MIB = 1 << 20
F32 = jnp.float32
BF16 = jnp.bfloat16


def project_kernel(steps, heads, chunk, fetch, *refs):
    x_from, kw_from, vw_from, gain_ref, out_ref = refs[:5]
    x_ref = refs[5] if fetch else x_from
    kw_ref, vw_ref, k_acc, v_acc, sems = refs[6 if fetch else 5 :]
    depth, width = kw_ref.shape
    tile = depth // steps
    columns = pl.ds(chunk * width, width)
    copies = []
    for step in range(steps):
        span = pl.ds(step * tile, tile)
        group = [
            pltpu.make_async_copy(kw_from.at[span, columns], kw_ref.at[span], sems.at[0, step]),
            pltpu.make_async_copy(vw_from.at[span, columns], vw_ref.at[span], sems.at[1, step]),
        ]
        if fetch:
            group.append(
                pltpu.make_async_copy(x_from.at[:, span], x_ref.at[:, span], sems.at[2, step])
            )
        for copy in group:
            copy.start()
        copies.append(group)
    for step in range(steps):
        for copy in copies[step]:
            copy.wait()
        span = slice(step * tile, (step + 1) * tile)
        x = x_ref[:, span]
        k_part = jnp.dot(x, kw_ref[span], preferred_element_type=F32)
        v_part = jnp.dot(x, vw_ref[span], preferred_element_type=F32)
        if step == 0:
            k_acc[...] = k_part
            v_acc[...] = v_part
        else:
            k_acc[...] += k_part
            v_acc[...] += v_part
    for head in range(heads):
        columns = slice(head * HD, (head + 1) * HD)
        raw = k_acc[:, columns]
        mean_square = jnp.mean(raw * raw, axis=1, keepdims=True)
        keys = raw / jnp.sqrt(mean_square + EPS) * gain_ref[...]
        out_ref[head, :, :HD] = keys.astype(BF16)
        out_ref[head, :, HD:] = v_acc[:, columns].astype(BF16)


def project(projected, key_weight, value_weight, gain, chunk, heads, held, keep):
    rows, depth = projected.shape
    steps = 8
    width = heads * HD
    fetch = held is None
    vmem = pl.BlockSpec(memory_space=pltpu.VMEM)
    hbm = pl.BlockSpec(memory_space=pltpu.HBM)
    shape = jax.ShapeDtypeStruct((heads, rows, 2 * HD), BF16)
    x_space = pltpu.VMEM((rows, depth), BF16)
    stay = functools.partial(pltpu.with_memory_space_constraint, memory_space=pltpu.HBM)
    key_weight, value_weight = stay(key_weight), stay(value_weight)
    if fetch:
        projected = stay(projected)
    result = pl.pallas_call(
        functools.partial(project_kernel, steps, heads, chunk, fetch),
        in_specs=[hbm if fetch else vmem, hbm, hbm, vmem],
        out_specs=(vmem, vmem) if keep else vmem,
        out_shape=(shape, x_space) if keep else shape,
        scratch_shapes=([x_space] if fetch and not keep else [])
        + [pltpu.VMEM((depth, width), BF16)] * 2
        + [pltpu.VMEM((rows, width), F32)] * 2
        + [pltpu.SemaphoreType.DMA((3, steps))],
        cost_estimate=pl.CostEstimate(
            flops=4 * rows * depth * width,
            bytes_accessed=2 * depth * (rows * fetch + 2 * width),
            transcendentals=0,
        ),
        compiler_params=pltpu.CompilerParams(vmem_limit_bytes=24 * MIB),
    )(projected if fetch else held, key_weight, value_weight, gain)
    return result if keep else (result, held)


def diagonal():
    rows = lax.broadcasted_iota(jnp.int32, (HD, HD), 0)
    lanes = lax.broadcasted_iota(jnp.int32, (HD, HD), 1)
    return rows == lanes


def to_lanes(column_block, eye):
    return jnp.sum(jnp.where(eye, column_block, 0.0), axis=0, keepdims=True)


def to_column(lane_row, eye):
    return jnp.sum(jnp.where(eye, lane_row, 0.0), axis=1, keepdims=True)


def split_rows(rows):
    high = rows.astype(BF16)
    rest = rows - high.astype(F32)
    middle = rest.astype(BF16)
    low = (rest - middle.astype(F32)).astype(BF16)
    return high, middle, low


def build_tables(heads, places, kv_refs, edges_ref, keys, values):
    sources = len(kv_refs)
    count = kv_refs[0].shape[1]
    section_count, block_count = lax.axis_size("section"), lax.axis_size("blk")
    section, row_block = lax.axis_index("section"), lax.axis_index("blk")
    values[:, :, HD:] = jnp.ones((heads, sources * count, HD), BF16)
    for source, kv in enumerate(kv_refs):
        other, back = places[source]
        place = lax.rem(section + section_count - back, section_count) * block_count
        base = (place + (row_block ^ other)) * count
        span = slice(source * count, (source + 1) * count)
        token = base + lax.broadcasted_iota(jnp.int32, (count, HD), 0)
        inside = (token >= edges_ref[0:1, :]) & (token < edges_ref[1:2, :])
        frame = jnp.where(inside, 1.0, 0.0).astype(BF16)
        for head in range(heads):
            keys[head, span, :HD] = kv[head, :, :HD]
            keys[head, span, HD:] = frame
            values[head, span, :HD] = kv[head, :, HD:]


def build_mask(other, sub_heads, first_ref, count_ref, mask):
    text_rows = first_ref.shape[1]
    row = lax.axis_index("blk") ^ other
    eye = diagonal()
    frame = lax.broadcasted_iota(jnp.int32, (HD, HD), 1).astype(F32)
    for start in range(0, text_rows, HD):
        span = slice(start, start + HD)
        first = to_column(first_ref[pl.ds(row, 1), span].astype(F32), eye)
        end = first + to_column(count_ref[pl.ds(row, 1), span].astype(F32), eye)
        seen = (frame >= first) & (frame < end) | (frame >= FRAMES)
        blocked = jnp.where(seen, 0.0, MASKED)[:, None, :]
        wide = jnp.broadcast_to(blocked, (HD, sub_heads, HD)).reshape(HD * sub_heads, HD)
        mask[start * sub_heads : (start + HD) * sub_heads, :] = wide.astype(BF16)


def attend_kernel(others, places, heads, *refs):
    group_count = len(others)
    q_refs, refs = refs[:group_count], refs[group_count:]
    (first_ref, count_ref, *refs), mask_refs = refs[:-1], refs[-1]
    if places:
        kv_refs, refs = refs[: len(places)], refs[len(places) :]
        edges_ref, *refs = refs
        out_refs, (keys, values, *buffers) = refs[:group_count], refs[group_count:]
        build_tables(keys.shape[0], places, kv_refs, edges_ref, keys, values)
    else:
        keys, values, *refs = refs
        out_refs, buffers = refs[:group_count], refs[group_count:]
    rows = q_refs[0].shape[0]
    total = keys.shape[1]
    tile = min(256, rows)
    block = math.gcd(512, total)
    for group, other in enumerate(others):
        build_mask(other, rows // first_ref.shape[1], first_ref, count_ref, mask_refs.at[group])

    eye = diagonal()
    tiles = [
        (group, head, start)
        for group in range(len(others))
        for head in heads
        for start in range(0, rows, tile)
    ]
    lane_rows = {}

    def load_query(index):
        group, head, start = tiles[index]
        span = slice(start, start + tile)
        columns = slice(head * HD, (head + 1) * HD)
        return jnp.concatenate([q_refs[group][span, columns], mask_refs[group, span, :]], axis=1)

    def score(index, begin, query):
        _, head, _ = tiles[index]
        span = slice(begin, begin + block)
        scores = lax.dot_general(
            query,
            keys[head, span],
            (((1,), (1,)), ((), ())),
            preferred_element_type=F32,
        )
        buffers[index % 2][:, span] = scores
        top = scores[:, :HD]
        for part in range(HD, block, HD):
            top = jnp.maximum(top, scores[:, part : part + HD])
        return top

    def weigh(index, begin, row_max):
        _, head, _ = tiles[index]
        span = slice(begin, begin + block)
        weights = jnp.exp2((buffers[index % 2][:, span] - row_max) * EXP_SCALE)
        return jnp.dot(
            weights.astype(BF16), values[head, span], preferred_element_type=F32
        )

    def store(index, summed, row_max):
        group, head, start = tiles[index]
        out_ref = out_refs[group]
        slot = heads.index(head)
        denominator = summed[:, HD:]
        out_ref[slot, start : start + tile, :] = (summed[:, :HD] / denominator).astype(
            out_ref.dtype
        )
        log_sum = row_max * EXP_SCALE + jnp.log2(denominator)
        lanes = lane_rows.setdefault((group, slot), [])
        for part in range(0, tile, HD):
            lanes.append(to_lanes(log_sum[part : part + HD], eye))
        if len(lanes) * HD == rows:
            store_lanes(out_ref, slot, rows, lanes)

    top = None
    query = load_query(0)
    for begin in range(0, total, block):
        part = score(0, begin, query)
        top = part if top is None else jnp.maximum(top, part)
    for index in range(len(tiles)):
        row_max = jnp.max(top, axis=1, keepdims=True)
        ahead = index + 1 < len(tiles)
        if ahead:
            query = load_query(index + 1)
        top = summed = None
        for begin in range(0, total, block):
            if ahead:
                part = score(index + 1, begin, query)
                top = part if top is None else jnp.maximum(top, part)
            part = weigh(index, begin, row_max)
            summed = part if summed is None else summed + part
        store(index, summed, row_max)


def store_lanes(out_ref, slot, rows, lane_rows):
    packed = out_ref.dtype == BF16
    flat = jnp.concatenate(lane_rows, axis=0)
    pieces = [flat]
    if packed:
        pieces = [piece.astype(F32) for piece in split_rows(flat)]
    pad = tail_rows(rows, packed) - len(pieces) * flat.shape[0]
    if pad:
        pieces.append(jnp.zeros((pad, HD), F32))
    out_ref[slot, rows:, :] = jnp.concatenate(pieces, axis=0).astype(out_ref.dtype)


def load_lanes(ref, slot, rows):
    flat = ref[slot, rows:, :].astype(F32)
    count = rows // HD
    if ref.dtype == BF16:
        return flat[:count] + flat[count : 2 * count] + flat[2 * count : 3 * count]
    return flat[:count]


def tail_rows(rows, packed):
    count = rows // HD
    if packed:
        return -(-3 * count // 16) * 16
    return -(-count // 8) * 8


def attend(groups, spans, tables, heads, kv_sources=None, edges=None, places=()):
    build = kv_sources is not None
    if build:
        table_heads, count, _ = kv_sources[0].shape
        total = len(kv_sources) * count
    else:
        total = tables[0].shape[1]
    rows = groups[0][0].shape[0]
    tile = min(256, rows)
    queries = [part for part, _, _ in groups]
    slots = len(heads)
    vmem = pl.BlockSpec(memory_space=pltpu.VMEM)
    inputs = [*queries, *spans]
    inputs += [*kv_sources, edges] if build else list(tables)
    in_specs = [vmem] * len(inputs)
    out_shape = [
        jax.ShapeDtypeStruct((slots, rows + tail_rows(rows, packed), HD), BF16 if packed else F32)
        for _, _, packed in groups
    ]
    if build:
        out_shape += [pltpu.VMEM((table_heads, total, 2 * HD), BF16)] * 2
    return pl.pallas_call(
        functools.partial(
            attend_kernel,
            tuple(other for _, other, _ in groups),
            tuple(places),
            tuple(heads),
        ),
        in_specs=in_specs,
        out_specs=[vmem] * len(out_shape),
        out_shape=out_shape,
        scratch_shapes=[pltpu.VMEM((tile, total), F32)] * 2
        + [pltpu.VMEM((len(groups), rows, HD), BF16)],
        cost_estimate=pl.CostEstimate(
            flops=8 * len(groups) * slots * rows * total * HD,
            bytes_accessed=slots * (total * 512 + len(groups) * rows * 512),
            transcendentals=len(groups) * slots * rows * total,
        ),
        compiler_params=pltpu.CompilerParams(vmem_limit_bytes=32 * MIB),
    )(*inputs)


def merge_lanes(lanes):
    top = functools.reduce(jnp.maximum, lanes)
    weights = [jnp.exp2(lane - top) for lane in lanes]
    total = functools.reduce(jnp.add, weights)
    return [weight / total for weight in weights], top + jnp.log2(total)


def merge_slot(refs, slots, rows, eye, write):
    lanes = [load_lanes(ref, slot, rows) for ref, slot in zip(refs, slots)]
    shares, merged_lanes = merge_lanes(lanes)
    for index in range(rows // HD):
        span = slice(index * HD, (index + 1) * HD)
        merged = None
        for ref, slot, share in zip(refs, slots, shares):
            part = to_column(share[index : index + 1], eye) * ref[slot, span, :].astype(F32)
            merged = part if merged is None else merged + part
        write(span, merged)
    return merged_lanes


def merge_kernel(rows, got_ref, own_ref, send_ref):
    eye = diagonal()
    for head in range(send_ref.shape[0]):

        def write(span, merged):
            send_ref[head, span, :] = merged.astype(BF16)

        lanes = merge_slot((got_ref, own_ref), (head, head), rows, eye, write)
        store_lanes(send_ref, head, rows, [lanes])


def merge(got, own, rows):
    return pl.pallas_call(
        functools.partial(merge_kernel, rows),
        out_shape=jax.ShapeDtypeStruct(got.shape, BF16),
        cost_estimate=pl.CostEstimate(
            flops=8 * own.size, bytes_accessed=8 * own.size, transcendentals=0
        ),
        compiler_params=pltpu.CompilerParams(vmem_limit_bytes=32 * MIB),
    )(got, own)


def slots_of(refs):
    return [(ref, head) for ref in refs for head in range(ref.shape[0])]


def gather_home_kernel(count, rows, *refs):
    out_ref = refs[-1]
    eye = diagonal()
    pairs = zip(slots_of(refs[:count]), slots_of(refs[count:-1]))
    for slot, ((own, own_head), (got, got_head)) in enumerate(pairs):

        def write(span, merged):
            out_ref[slot, span, :] = merged

        lanes = merge_slot((own, got), (own_head, got_head), rows, eye, write)
        store_lanes(out_ref, slot, rows, [lanes])


def gather_home(own, received, rows):
    slots = sum(part.shape[0] for part in own)
    return pl.pallas_call(
        functools.partial(gather_home_kernel, len(own), rows),
        out_shape=jax.ShapeDtypeStruct((slots, *own[0].shape[1:]), F32),
        cost_estimate=pl.CostEstimate(
            flops=8 * slots * rows * HD, bytes_accessed=8 * slots * rows * HD, transcendentals=0
        ),
        compiler_params=pltpu.CompilerParams(vmem_limit_bytes=32 * MIB),
        name="gather_home",
    )(*own, *received)


def finish_kernel(rows, own_ref, *refs):
    out_ref = refs[-1]
    eye = diagonal()
    sub_heads = out_ref.shape[1]
    for slot, (got, got_head) in enumerate(slots_of(refs[:-1])):
        columns = slice(slot * HD, (slot + 1) * HD)

        def write(span, merged):
            texts = slice(span.start // sub_heads, span.stop // sub_heads)
            out_ref[texts, :, columns] = merged.reshape(-1, sub_heads, HD).astype(BF16)

        merge_slot((own_ref, got), (slot, got_head), rows, eye, write)


def finish(own, received, rows, shape):
    return pl.pallas_call(
        functools.partial(finish_kernel, rows),
        out_shape=jax.ShapeDtypeStruct(shape, BF16),
        cost_estimate=pl.CostEstimate(
            flops=8 * own.size, bytes_accessed=8 * own.size, transcendentals=0
        ),
        compiler_params=pltpu.CompilerParams(vmem_limit_bytes=32 * MIB),
        name="finish",
    )(own, *received)


def frame_starts(frame_tokens):
    ids = jnp.arange(FRAMES, dtype=jnp.int32)
    before = jnp.where(ids[:, None] < ids[None, :], frame_tokens[:, None], 0)
    return jnp.sum(before, axis=0)


def body(
    projected, key_weight, value_weight, key_gain, queries, frame_tokens, span_first, span_count
):
    own_rows, sub_heads, width = queries.shape
    local_heads = width // HD
    chunk_heads = 2 if local_heads % 2 == 0 else 1
    chunks = local_heads // chunk_heads
    section_count = lax.axis_size("section")
    block_count = lax.axis_size("blk")
    bits = block_count.bit_length() - 1
    far = 1 << (bits - 1)
    lower = [1 << bit for bit in range(bits - 1)]
    near = [lower[(c + 1) % 2] for c in range(chunks)]
    middle = [[bit for bit in lower if bit != near[c]] for c in range(chunks)]

    def across(x, bit):
        return lax.ppermute(x, "blk", [(i, i ^ bit) for i in range(block_count)])

    def across_section(x):
        return lax.ppermute(
            x, "section", [(i, (i + 1) % section_count) for i in range(section_count)]
        )

    rows = own_rows * sub_heads
    chunk_width = chunk_heads * HD
    own_queries = [
        queries[:, :, c * chunk_width : (c + 1) * chunk_width].reshape(rows, chunk_width)
        for c in range(chunks)
    ]
    far_queries, near_queries, near_far_queries = [], [], []
    for c in range(chunks):
        far_queries.append(across(own_queries[c], far))
        near_queries.append(across(own_queries[c], near[c]))
    for c in range(chunks):
        near_far_queries.append(across(far_queries[c], near[c]))

    gain = key_gain.reshape(1, HD)

    received = []
    held = None
    for c in range(chunks):
        own, held = project(
            projected, key_weight, value_weight, gain, c, chunk_heads, held, chunks > 1 and c == 0
        )
        if c == chunks - 1:
            own, frame_tokens = lax.optimization_barrier((own, frame_tokens))
        plane = [own]
        for bit in middle[c]:
            plane = plane + [across(part, bit) for part in plane]
        kv_sources = []
        for part in plane:
            kv_sources.append(part)
            if section_count > 1:
                kv_sources.append(across_section(part))
        received.append(kv_sources)

    starts = frame_starts(frame_tokens)
    places = []
    for c in range(chunks):
        source_bits = [0]
        for bit in middle[c]:
            source_bits = source_bits + [other ^ bit for other in source_bits]
        places.append([(other, s) for other in source_bits for s in range(section_count)])
    edges = jnp.pad(jnp.stack([starts, starts + frame_tokens]), ((0, 0), (0, HD - FRAMES)))
    spans = [span_first.reshape(-1, own_rows), span_count.reshape(-1, own_rows)]

    homes, got_home, got_back = [], [], []
    for c in range(chunks):
        every = tuple(range(chunk_heads))
        pieces = [(head,) for head in every] if c == chunks - 1 else [every]
        tables = None
        got_corner = []
        for heads in pieces:
            corner, *built = attend(
                [(near_far_queries[c], near[c] ^ far, True)],
                spans,
                tables,
                heads,
                None if tables else received[c],
                edges,
                () if tables else places[c],
            )
            tables = tables or built
            got_corner.append(across(corner, near[c]))
        far_group = (far_queries[c], far, False)
        near_group = (near_queries[c], near[c], True)
        for index, heads in enumerate(pieces):
            both = len(pieces) == 1
            far_side, *near_sides = attend(
                [far_group, near_group] if both else [far_group], spans, tables, heads
            )
            send = merge(got_corner[index], far_side, rows)
            got_back.append(across(send, far))
        if not near_sides:
            near_sides = attend([near_group], spans, tables, every)
        got_home.append(across(near_sides[0], near[c]))
        homes += attend([(own_queries[c], 0, False)], spans, tables, every)
    home = gather_home(homes, got_home, rows)
    return finish(home, got_back, rows, queries.shape)


def solution(mesh):
    placed = (
        P(("section", "blk"), None),
        P(None, "head"),
        P(None, "head"),
        P(),
        P("blk", "section", "head"),
        P(),
        P(),
        P(),
    )
    return jax.shard_map(
        body,
        mesh=mesh,
        in_specs=placed,
        out_specs=P("blk", "section", "head"),
        check_vma=False,
    )
```

```python
import functools
import math

import jax
import jax.numpy as jnp
from jax import lax
from jax.experimental import pallas as pl
from jax.experimental.pallas import tpu as pltpu
from jax.sharding import PartitionSpec as P


HD = 128
FRAMES = 32
EPS = 1e-05
MASKED = -1e30
EXP_SCALE = math.log2(math.e) * HD ** (-0.5)
MIB = 1 << 20
F32 = jnp.float32
BF16 = jnp.bfloat16


def project_kernel(steps, heads, chunk, fetch, *refs):
    x_from, kw_from, vw_from, gain_ref, out_ref = refs[:5]
    x_ref = refs[5] if fetch else x_from
    kw_ref, vw_ref, k_acc, v_acc, sems = refs[6 if fetch else 5 :]
    depth, width = kw_ref.shape
    tile = depth // steps
    columns = pl.ds(chunk * width, width)
    copies = []
    for step in range(steps):
        span = pl.ds(step * tile, tile)
        group = [
            pltpu.make_async_copy(kw_from.at[span, columns], kw_ref.at[span], sems.at[0, step]),
            pltpu.make_async_copy(vw_from.at[span, columns], vw_ref.at[span], sems.at[1, step]),
        ]
        if fetch:
            group.append(
                pltpu.make_async_copy(x_from.at[:, span], x_ref.at[:, span], sems.at[2, step])
            )
        for copy in group:
            copy.start()
        copies.append(group)
    for step in range(steps):
        for copy in copies[step]:
            copy.wait()
        span = slice(step * tile, (step + 1) * tile)
        x = x_ref[:, span]
        k_part = jnp.dot(x, kw_ref[span], preferred_element_type=F32)
        v_part = jnp.dot(x, vw_ref[span], preferred_element_type=F32)
        if step == 0:
            k_acc[...] = k_part
            v_acc[...] = v_part
        else:
            k_acc[...] += k_part
            v_acc[...] += v_part
    for head in range(heads):
        columns = slice(head * HD, (head + 1) * HD)
        raw = k_acc[:, columns]
        mean_square = jnp.mean(raw * raw, axis=1, keepdims=True)
        keys = raw / jnp.sqrt(mean_square + EPS) * gain_ref[...]
        out_ref[head, :, :HD] = keys.astype(BF16)
        out_ref[head, :, HD:] = v_acc[:, columns].astype(BF16)


def project(projected, key_weight, value_weight, gain, chunk, heads, held, keep):
    rows, depth = projected.shape
    steps = 8
    width = heads * HD
    fetch = held is None
    vmem = pl.BlockSpec(memory_space=pltpu.VMEM)
    hbm = pl.BlockSpec(memory_space=pltpu.HBM)
    shape = jax.ShapeDtypeStruct((heads, rows, 2 * HD), BF16)
    x_space = pltpu.VMEM((rows, depth), BF16)
    stay = functools.partial(pltpu.with_memory_space_constraint, memory_space=pltpu.HBM)
    key_weight, value_weight = stay(key_weight), stay(value_weight)
    if fetch:
        projected = stay(projected)
    result = pl.pallas_call(
        functools.partial(project_kernel, steps, heads, chunk, fetch),
        in_specs=[hbm if fetch else vmem, hbm, hbm, vmem],
        out_specs=(vmem, vmem) if keep else vmem,
        out_shape=(shape, x_space) if keep else shape,
        scratch_shapes=([x_space] if fetch and not keep else [])
        + [pltpu.VMEM((depth, width), BF16)] * 2
        + [pltpu.VMEM((rows, width), F32)] * 2
        + [pltpu.SemaphoreType.DMA((3, steps))],
        cost_estimate=pl.CostEstimate(
            flops=4 * rows * depth * width,
            bytes_accessed=2 * depth * (rows * fetch + 2 * width),
            transcendentals=0,
        ),
        compiler_params=pltpu.CompilerParams(vmem_limit_bytes=24 * MIB),
    )(projected if fetch else held, key_weight, value_weight, gain)
    return result if keep else (result, held)


def diagonal():
    rows = lax.broadcasted_iota(jnp.int32, (HD, HD), 0)
    lanes = lax.broadcasted_iota(jnp.int32, (HD, HD), 1)
    return rows == lanes


def to_lanes(column_block, eye):
    return jnp.sum(jnp.where(eye, column_block, 0.0), axis=0, keepdims=True)


def to_column(lane_row, eye):
    return jnp.sum(jnp.where(eye, lane_row, 0.0), axis=1, keepdims=True)


def split_rows(rows):
    high = rows.astype(BF16)
    rest = rows - high.astype(F32)
    middle = rest.astype(BF16)
    low = (rest - middle.astype(F32)).astype(BF16)
    return high, middle, low


def build_tables(heads, places, kv_refs, edges_ref, keys, values):
    sources = len(kv_refs)
    count = kv_refs[0].shape[1]
    section_count, block_count = lax.axis_size("section"), lax.axis_size("blk")
    section, row_block = lax.axis_index("section"), lax.axis_index("blk")
    values[:, :, HD:] = jnp.ones((heads, sources * count, HD), BF16)
    for source, kv in enumerate(kv_refs):
        other, back = places[source]
        place = lax.rem(section + section_count - back, section_count) * block_count
        base = (place + (row_block ^ other)) * count
        span = slice(source * count, (source + 1) * count)
        token = base + lax.broadcasted_iota(jnp.int32, (count, HD), 0)
        inside = (token >= edges_ref[0:1, :]) & (token < edges_ref[1:2, :])
        frame = jnp.where(inside, 1.0, 0.0).astype(BF16)
        for head in range(heads):
            keys[head, span, :HD] = kv[head, :, :HD]
            keys[head, span, HD:] = frame
            values[head, span, :HD] = kv[head, :, HD:]


def build_mask(other, sub_heads, first_ref, count_ref, mask):
    text_rows = first_ref.shape[1]
    row = lax.axis_index("blk") ^ other
    eye = diagonal()
    frame = lax.broadcasted_iota(jnp.int32, (HD, HD), 1).astype(F32)
    for start in range(0, text_rows, HD):
        span = slice(start, start + HD)
        first = to_column(first_ref[pl.ds(row, 1), span].astype(F32), eye)
        end = first + to_column(count_ref[pl.ds(row, 1), span].astype(F32), eye)
        seen = (frame >= first) & (frame < end) | (frame >= FRAMES)
        blocked = jnp.where(seen, 0.0, MASKED)[:, None, :]
        wide = jnp.broadcast_to(blocked, (HD, sub_heads, HD)).reshape(HD * sub_heads, HD)
        mask[start * sub_heads : (start + HD) * sub_heads, :] = wide.astype(BF16)


def attend_kernel(others, places, heads, *refs):
    group_count = len(others)
    q_refs, refs = refs[:group_count], refs[group_count:]
    (first_ref, count_ref, *refs), mask_refs = refs[:-1], refs[-1]
    if places:
        kv_refs, refs = refs[: len(places)], refs[len(places) :]
        edges_ref, *refs = refs
        out_refs, (keys, values, *buffers) = refs[:group_count], refs[group_count:]
        build_tables(keys.shape[0], places, kv_refs, edges_ref, keys, values)
    else:
        keys, values, *refs = refs
        out_refs, buffers = refs[:group_count], refs[group_count:]
    rows = q_refs[0].shape[0]
    total = keys.shape[1]
    tile = min(256, rows)
    block = math.gcd(512, total)
    for group, other in enumerate(others):
        build_mask(other, rows // first_ref.shape[1], first_ref, count_ref, mask_refs.at[group])

    eye = diagonal()
    tiles = [
        (group, head, start)
        for group in range(len(others))
        for head in heads
        for start in range(0, rows, tile)
    ]
    lane_rows = {}

    def load_query(index):
        group, head, start = tiles[index]
        span = slice(start, start + tile)
        columns = slice(head * HD, (head + 1) * HD)
        return jnp.concatenate([q_refs[group][span, columns], mask_refs[group, span, :]], axis=1)

    def score(index, begin, query):
        _, head, _ = tiles[index]
        span = slice(begin, begin + block)
        scores = lax.dot_general(
            query,
            keys[head, span],
            (((1,), (1,)), ((), ())),
            preferred_element_type=F32,
        )
        buffers[index % 2][:, span] = scores
        top = scores[:, :HD]
        for part in range(HD, block, HD):
            top = jnp.maximum(top, scores[:, part : part + HD])
        return top

    def weigh(index, begin, row_max):
        _, head, _ = tiles[index]
        span = slice(begin, begin + block)
        weights = jnp.exp2((buffers[index % 2][:, span] - row_max) * EXP_SCALE)
        return jnp.dot(
            weights.astype(BF16), values[head, span], preferred_element_type=F32
        )

    def store(index, summed, row_max):
        group, head, start = tiles[index]
        out_ref = out_refs[group]
        slot = heads.index(head)
        denominator = summed[:, HD:]
        out_ref[slot, start : start + tile, :] = (summed[:, :HD] / denominator).astype(
            out_ref.dtype
        )
        log_sum = row_max * EXP_SCALE + jnp.log2(denominator)
        lanes = lane_rows.setdefault((group, slot), [])
        for part in range(0, tile, HD):
            lanes.append(to_lanes(log_sum[part : part + HD], eye))
        if len(lanes) * HD == rows:
            store_lanes(out_ref, slot, rows, lanes)

    top = None
    query = load_query(0)
    for begin in range(0, total, block):
        part = score(0, begin, query)
        top = part if top is None else jnp.maximum(top, part)
    for index in range(len(tiles)):
        row_max = jnp.max(top, axis=1, keepdims=True)
        ahead = index + 1 < len(tiles)
        if ahead:
            query = load_query(index + 1)
        top = summed = None
        for begin in range(0, total, block):
            if ahead:
                part = score(index + 1, begin, query)
                top = part if top is None else jnp.maximum(top, part)
            part = weigh(index, begin, row_max)
            summed = part if summed is None else summed + part
        store(index, summed, row_max)


def store_lanes(out_ref, slot, rows, lane_rows):
    packed = out_ref.dtype == BF16
    flat = jnp.concatenate(lane_rows, axis=0)
    pieces = [flat]
    if packed:
        pieces = [piece.astype(F32) for piece in split_rows(flat)]
    pad = tail_rows(rows, packed) - len(pieces) * flat.shape[0]
    if pad:
        pieces.append(jnp.zeros((pad, HD), F32))
    out_ref[slot, rows:, :] = jnp.concatenate(pieces, axis=0).astype(out_ref.dtype)


def load_lanes(ref, slot, rows):
    flat = ref[slot, rows:, :].astype(F32)
    count = rows // HD
    if ref.dtype == BF16:
        return flat[:count] + flat[count : 2 * count] + flat[2 * count : 3 * count]
    return flat[:count]


def tail_rows(rows, packed):
    count = rows // HD
    if packed:
        return -(-3 * count // 16) * 16
    return -(-count // 8) * 8


def attend(groups, spans, tables, heads, kv_sources=None, edges=None, places=()):
    build = kv_sources is not None
    if build:
        table_heads, count, _ = kv_sources[0].shape
        total = len(kv_sources) * count
    else:
        total = tables[0].shape[1]
    rows = groups[0][0].shape[0]
    tile = min(256, rows)
    queries = [part for part, _, _ in groups]
    slots = len(heads)
    vmem = pl.BlockSpec(memory_space=pltpu.VMEM)
    inputs = [*queries, *spans]
    inputs += [*kv_sources, edges] if build else list(tables)
    in_specs = [vmem] * len(inputs)
    out_shape = [
        jax.ShapeDtypeStruct((slots, rows + tail_rows(rows, packed), HD), BF16 if packed else F32)
        for _, _, packed in groups
    ]
    if build:
        out_shape += [pltpu.VMEM((table_heads, total, 2 * HD), BF16)] * 2
    return pl.pallas_call(
        functools.partial(
            attend_kernel,
            tuple(other for _, other, _ in groups),
            tuple(places),
            tuple(heads),
        ),
        in_specs=in_specs,
        out_specs=[vmem] * len(out_shape),
        out_shape=out_shape,
        scratch_shapes=[pltpu.VMEM((tile, total), F32)] * 2
        + [pltpu.VMEM((len(groups), rows, HD), BF16)],
        cost_estimate=pl.CostEstimate(
            flops=8 * len(groups) * slots * rows * total * HD,
            bytes_accessed=slots * (total * 512 + len(groups) * rows * 512),
            transcendentals=len(groups) * slots * rows * total,
        ),
        compiler_params=pltpu.CompilerParams(vmem_limit_bytes=32 * MIB),
    )(*inputs)


def merge_lanes(lanes):
    top = functools.reduce(jnp.maximum, lanes)
    weights = [jnp.exp2(lane - top) for lane in lanes]
    total = functools.reduce(jnp.add, weights)
    return [weight / total for weight in weights], top + jnp.log2(total)


def merge_slot(refs, slots, rows, eye, write):
    lanes = [load_lanes(ref, slot, rows) for ref, slot in zip(refs, slots)]
    shares, merged_lanes = merge_lanes(lanes)
    for index in range(rows // HD):
        span = slice(index * HD, (index + 1) * HD)
        merged = None
        for ref, slot, share in zip(refs, slots, shares):
            part = to_column(share[index : index + 1], eye) * ref[slot, span, :].astype(F32)
            merged = part if merged is None else merged + part
        write(span, merged)
    return merged_lanes


def merge_kernel(rows, got_ref, own_ref, send_ref):
    eye = diagonal()
    for head in range(send_ref.shape[0]):

        def write(span, merged):
            send_ref[head, span, :] = merged.astype(BF16)

        lanes = merge_slot((got_ref, own_ref), (head, head), rows, eye, write)
        store_lanes(send_ref, head, rows, [lanes])


def merge(got, own, rows):
    return pl.pallas_call(
        functools.partial(merge_kernel, rows),
        out_shape=jax.ShapeDtypeStruct(got.shape, BF16),
        cost_estimate=pl.CostEstimate(
            flops=8 * own.size, bytes_accessed=8 * own.size, transcendentals=0
        ),
        compiler_params=pltpu.CompilerParams(vmem_limit_bytes=32 * MIB),
    )(got, own)


def slots_of(refs):
    return [(ref, head) for ref in refs for head in range(ref.shape[0])]


def gather_home_kernel(count, rows, *refs):
    out_ref = refs[-1]
    eye = diagonal()
    pairs = zip(slots_of(refs[:count]), slots_of(refs[count:-1]))
    for slot, ((own, own_head), (got, got_head)) in enumerate(pairs):

        def write(span, merged):
            out_ref[slot, span, :] = merged

        lanes = merge_slot((own, got), (own_head, got_head), rows, eye, write)
        store_lanes(out_ref, slot, rows, [lanes])


def gather_home(own, received, rows):
    slots = sum(part.shape[0] for part in own)
    return pl.pallas_call(
        functools.partial(gather_home_kernel, len(own), rows),
        out_shape=jax.ShapeDtypeStruct((slots, *own[0].shape[1:]), F32),
        cost_estimate=pl.CostEstimate(
            flops=8 * slots * rows * HD, bytes_accessed=8 * slots * rows * HD, transcendentals=0
        ),
        compiler_params=pltpu.CompilerParams(vmem_limit_bytes=32 * MIB),
        name="gather",
    )(*own, *received)


def finish_kernel(rows, own_ref, *refs):
    out_ref = refs[-1]
    eye = diagonal()
    sub_heads = out_ref.shape[1]
    for slot, (got, got_head) in enumerate(slots_of(refs[:-1])):
        columns = slice(slot * HD, (slot + 1) * HD)

        def write(span, merged):
            texts = slice(span.start // sub_heads, span.stop // sub_heads)
            out_ref[texts, :, columns] = merged.reshape(-1, sub_heads, HD).astype(BF16)

        merge_slot((own_ref, got), (slot, got_head), rows, eye, write)


def finish(own, received, rows, shape):
    return pl.pallas_call(
        functools.partial(finish_kernel, rows),
        out_shape=jax.ShapeDtypeStruct(shape, BF16),
        cost_estimate=pl.CostEstimate(
            flops=8 * own.size, bytes_accessed=8 * own.size, transcendentals=0
        ),
        compiler_params=pltpu.CompilerParams(vmem_limit_bytes=32 * MIB),
        name="finish",
    )(own, *received)


def frame_starts(frame_tokens):
    ids = jnp.arange(FRAMES, dtype=jnp.int32)
    before = jnp.where(ids[:, None] < ids[None, :], frame_tokens[:, None], 0)
    return jnp.sum(before, axis=0)


def body(
    projected, key_weight, value_weight, key_gain, queries, frame_tokens, span_first, span_count
):
    own_rows, sub_heads, width = queries.shape
    local_heads = width // HD
    chunk_heads = 2 if local_heads % 2 == 0 else 1
    chunks = local_heads // chunk_heads
    section_count = lax.axis_size("section")
    block_count = lax.axis_size("blk")
    bits = block_count.bit_length() - 1
    far = 1 << (bits - 1)
    lower = [1 << bit for bit in range(bits - 1)]
    near = [lower[(c + 1) % 2] for c in range(chunks)]
    middle = [[bit for bit in lower if bit != near[c]] for c in range(chunks)]

    def across(x, bit):
        return lax.ppermute(x, "blk", [(i, i ^ bit) for i in range(block_count)])

    def across_section(x):
        return lax.ppermute(
            x, "section", [(i, (i + 1) % section_count) for i in range(section_count)]
        )

    rows = own_rows * sub_heads
    chunk_width = chunk_heads * HD
    own_queries = [
        queries[:, :, c * chunk_width : (c + 1) * chunk_width].reshape(rows, chunk_width)
        for c in range(chunks)
    ]
    own_queries = lax.optimization_barrier(own_queries)
    far_queries, near_queries, near_far_queries = [], [], []
    for c in range(chunks):
        far_queries.append(across(own_queries[c], far))
        near_queries.append(across(own_queries[c], near[c]))
    for c in range(chunks):
        near_far_queries.append(across(far_queries[c], near[c]))

    gain = key_gain.reshape(1, HD)

    received = []
    held = None
    for c in range(chunks):
        own, held = project(
            projected, key_weight, value_weight, gain, c, chunk_heads, held, chunks > 1 and c == 0
        )
        if c == chunks - 1:
            own, frame_tokens = lax.optimization_barrier((own, frame_tokens))
        plane = [own]
        for bit in middle[c]:
            plane = plane + [across(part, bit) for part in plane]
        kv_sources = []
        for part in plane:
            kv_sources.append(part)
            if section_count > 1:
                kv_sources.append(across_section(part))
        received.append(kv_sources)

    starts = frame_starts(frame_tokens)
    places = []
    for c in range(chunks):
        source_bits = [0]
        for bit in middle[c]:
            source_bits = source_bits + [other ^ bit for other in source_bits]
        places.append([(other, s) for other in source_bits for s in range(section_count)])
    edges = jnp.pad(jnp.stack([starts, starts + frame_tokens]), ((0, 0), (0, HD - FRAMES)))
    spans = [span_first.reshape(-1, own_rows), span_count.reshape(-1, own_rows)]

    homes, got_home, got_back = [], [], []
    for c in range(chunks):
        every = tuple(range(chunk_heads))
        pieces = [(head,) for head in every] if c == chunks - 1 else [every]
        tables = None
        got_corner = []
        for heads in pieces:
            corner, *built = attend(
                [(near_far_queries[c], near[c] ^ far, True)],
                spans,
                tables,
                heads,
                None if tables else received[c],
                edges,
                () if tables else places[c],
            )
            tables = tables or built
            got_corner.append(across(corner, near[c]))
        far_group = (far_queries[c], far, False)
        near_group = (near_queries[c], near[c], True)
        for index, heads in enumerate(pieces):
            both = len(pieces) == 1
            far_side, *near_sides = attend(
                [far_group, near_group] if both else [far_group], spans, tables, heads
            )
            send = merge(got_corner[index], far_side, rows)
            got_back.append(across(send, far))
        if not near_sides:
            near_sides = attend([near_group], spans, tables, every)
        got_home.append(across(near_sides[0], near[c]))
        homes += attend([(own_queries[c], 0, False)], spans, tables, every)
    home = gather_home(homes, got_back, rows)
    return finish(home, got_home, rows, queries.shape)


def solution(mesh):
    placed = (
        P(("section", "blk"), None),
        P(None, "head"),
        P(None, "head"),
        P(),
        P("blk", "section", "head"),
        P(),
        P(),
        P(),
    )
    return jax.shard_map(
        body,
        mesh=mesh,
        in_specs=placed,
        out_specs=P("blk", "section", "head"),
        check_vma=False,
    )
```
